32 devices in a mesh: gx: 2 (over y), gy: 4 (over x, core), gz: 4 (over z).
Axes of the slice: x: 2, y: 2, z: 4, core: 2. Of those that a mesh axis runs over, the one named last changes fastest.
Arguments:
- direction: float32 [3, 32, 32, 512], P(None, 'gx', 'gy', 'gz'), may hold values from -6 to 6
- base_flow: bfloat16 [2, 3, 32, 32, 512], P(None, None, 'gx', 'gy', 'gz'), may hold values from -4 to 4
- local_inv: float32 [32, 16], P('gx'), may hold values from -1.5 to 1.5
- couple_in: float32 [4, 16], P('gx'), may hold values from -1.5 to 1.5
- couple_out: float32 [32, 2], P('gx'), may hold values from -4 to 4
- schur_inv: float32 [4, 4], replicated, may hold values from -3 to 3
- plane_x: int32 [8], replicated, may hold values from 0 to 31, as said below
- slot_plane: int32 [8], replicated, may hold values from 0 to 7, each once
- window_inv: float32 [8, 4, 4, 16, 16], P('gx', 'gy', 'gz'), may hold values from -4 to 20
Outputs:
- hess_vec: float32 [3, 32, 32, 512], P(None, 'gx', 'gy', 'gz')
The draws below stay inside these ranges and needn't reach their ends.
Inputs may be any that keep to these rules, and one draw needn't show every extreme that they name: `plane_x`: each plane lies on a streamwise cell of the grid; the planes lie on distinct cells; at most 8 of them lie in the cells of one index d of gx (cells d*16 to d*16 + 15), and some index holds exactly 8.
All inputs are finite; a program needn't handle non-finite values.
Results may differ from the reference program's by a relative error of at most 0.0003.
Values sent between devices are 32-bit elements; how exact they have to be, the bound alone decides.
A program may use at most 64 MiB of HBM per device.

```python
import math
import jax
import jax.numpy as jnp
from jax import lax

CX = 16
CY = 8
WIN = 8
NP = 8
PMAX = 8
NI = 4
CZW = 16
NX = 32
NY = 32
NZ = 512
N_GX = 2
N_GY = 4
N_GZ = 4


def shuffle_cells(device_key):
    return jax.random.permutation(device_key, CX)


def draw_plane_x(key, part):
    start_key, order_key, place_key = jax.random.split(key, 3)
    busiest = jax.random.randint(start_key, (), 0, N_GX)
    plane_order = jax.random.permutation(order_key, NP)
    device_keys = jax.random.split(place_key, N_GX)
    offsets = jax.vmap(shuffle_cells)(device_keys)
    devices = jnp.arange(N_GX, dtype=jnp.int32)[:, None]
    slot_index = jnp.arange(PMAX, dtype=jnp.int32)[None, :]
    shifted = (devices - busiest - 1) % N_GX
    other_rank = PMAX + shifted + slot_index * (N_GX - 1)
    plane_rank = jnp.where(devices == busiest, slot_index, other_rank)
    filled = plane_rank < NP
    plane_id = jnp.where(filled, plane_order[jnp.minimum(plane_rank, NP - 1)], NP)
    cell_x = devices * CX + offsets[:, :PMAX]
    result = jnp.zeros((NP,), jnp.int32)
    return result.at[plane_id.reshape(-1)].set(cell_x.reshape(-1).astype(jnp.int32), mode='drop')


def draw_window_inv(key, part):
    diag_key, rest_key = jax.random.split(key)
    full_shape = (NP, N_GY, N_GZ, CZW, CZW)
    spread_part = jnp.clip(jax.random.normal(rest_key, full_shape, jnp.float32), -4.0, 4.0)
    levels = jnp.exp(jax.random.uniform(diag_key, full_shape, jnp.float32, minval=math.log(4.0), maxval=math.log(16.0)))
    identity_block = jnp.eye(CZW, dtype=jnp.float32)
    return spread_part + identity_block * levels


def shard_levels(stream_key, dims, cuts, low, largest):
    level = 1.0
    for position, shards_of in cuts:
        steps = jax.random.uniform(jax.random.fold_in(jax.random.fold_in(stream_key, 6), position), (shards_of,), jnp.float32, low / len(cuts), largest / len(cuts))
        level = level * jnp.repeat(jnp.exp(steps), dims[position] // shards_of).reshape((-1,) + (1,) * (len(dims) - 1 - position))
    return level


def scatter_about(own_key, extent, width, limit, shards=(), kind=jnp.bfloat16):
    values = width * jax.random.normal(own_key, extent, jnp.float32)
    if shards:
        values = values * shard_levels(own_key, extent, shards, -0.22, 0.18)
    return jnp.clip(values, -limit, limit).astype(kind)


def setup_inputs(seed: int = 0) -> dict:
    splits = jax.random.split(jax.random.key(seed), 10)
    return {
        "direction": scatter_about(splits[0], (3, NX, NY, NZ), 1.0, 6.0, ((1, 2), (2, 4), (3, 4)), jnp.float32),
        "base_flow": scatter_about(splits[1], (2, 3, NX, NY, NZ), 1.0, 4.0, ((2, 2), (3, 4), (4, 4))),
        "local_inv": scatter_about(splits[2], (NX, CX), CX ** -0.5, 1.5, ((0, 2),), jnp.float32),
        "couple_in": scatter_about(splits[3], (NI, CX), CX ** -0.5, 1.5, ((0, 2),), jnp.float32),
        "couple_out": scatter_about(splits[4], (NX, 2), 2 ** -0.5, 4.0, ((0, 2),), jnp.float32),
        "schur_inv": scatter_about(splits[5], (NI, NI), NI ** -0.5, 3.0, (), jnp.float32),
        "plane_x": draw_plane_x(jax.random.fold_in(splits[9], 71), 0),
        "slot_plane": jax.random.permutation(splits[7], NP).astype(jnp.int32),
        "window_inv": draw_window_inv(jax.random.fold_in(splits[9], 71), 0),
    }


time_step = 0.15
high = lax.Precision.HIGHEST


def stencil_x(field):
    length = field.shape[1]
    padded = jnp.pad(field, ((0, 0), (2, 2), (0, 0), (0, 0)))
    near_diff = padded[:, 3:length + 3] - padded[:, 1:length + 1]
    far_diff = padded[:, 4:length + 4] - padded[:, 0:length]
    return (7.0 / 9.0) * near_diff + (1.0 / 36.0) * far_diff


def central_six(field, axis_index):
    def shifted(offset):
        return jnp.roll(field, -offset, axis=axis_index)
    return (45.0 * (shifted(1) - shifted(-1)) - 9.0 * (shifted(2) - shifted(-2)) + (shifted(3) - shifted(-3))) / 60.0


def solve_x(rhs, local_inv, couple_in, couple_out, schur_inv):
    blocks = rhs.reshape(3, N_GX, CX, NY, NZ)
    inverse_blocks = local_inv.reshape(N_GX, CX, CX)
    in_blocks = couple_in.reshape(N_GX, 2, CX)
    out_blocks = couple_out.reshape(N_GX, CX, 2)
    local_part = jnp.einsum('pij,cpjyz->cpiyz', inverse_blocks, blocks, precision=high)
    edge_values = jnp.einsum('pkj,cpjyz->cpkyz', in_blocks, blocks, precision=high).reshape(3, NI, NY, NZ)
    solved = jnp.einsum('mn,cnyz->cmyz', schur_inv, edge_values, precision=high).reshape(3, N_GX, 2, NY, NZ)
    result = local_part + jnp.einsum('pik,cpkyz->cpiyz', out_blocks, solved, precision=high)
    return result.reshape(3, NX, NY, NZ)


def solve_x_adjoint(grad_in, local_inv, couple_in, couple_out, schur_inv):
    blocks = grad_in.reshape(3, N_GX, CX, NY, NZ)
    inverse_blocks = local_inv.reshape(N_GX, CX, CX)
    in_blocks = couple_in.reshape(N_GX, 2, CX)
    out_blocks = couple_out.reshape(N_GX, CX, 2)
    local_part = jnp.einsum('pji,cpjyz->cpiyz', inverse_blocks, blocks, precision=high)
    edge_values = jnp.einsum('pik,cpiyz->cpkyz', out_blocks, blocks, precision=high).reshape(3, NI, NY, NZ)
    solved = jnp.einsum('nm,cnyz->cmyz', schur_inv, edge_values, precision=high).reshape(3, N_GX, 2, NY, NZ)
    result = local_part + jnp.einsum('pki,cpkyz->cpiyz', in_blocks, solved, precision=high)
    return result.reshape(3, NX, NY, NZ)


def observe(state, plane_x, slot_plane, window_inv):
    picked = state[:, plane_x]
    windows = picked.reshape(3, NP, NY, NZ // WIN, WIN).mean(axis=4)
    by_slot = windows[:, slot_plane].reshape(3, NP, N_GY, CY, N_GZ, CZW)
    weighted = jnp.einsum('jgsab,cjgysb->cjgysa', window_inv, by_slot, precision=high).reshape(3, NP, NY, NZ // WIN)
    by_plane = jnp.zeros_like(weighted).at[:, slot_plane].set(weighted)
    expanded = jnp.repeat(by_plane, WIN, axis=3) / WIN
    return jnp.zeros_like(state).at[:, plane_x].add(expanded)


def reference(direction, base_flow, local_inv, couple_in, couple_out, schur_inv, plane_x, slot_plane, window_inv):
    matrices = (local_inv, couple_in, couple_out, schur_inv)

    def tangent(state, step_base):
        velocity = step_base.astype(jnp.float32)
        slope_x = solve_x(stencil_x(state), *matrices)
        slope_y = central_six(state, 2)
        slope_z = central_six(state, 3)
        return state - time_step * (velocity[0] * slope_x + velocity[1] * slope_y + velocity[2] * slope_z)

    def adjoint(state, step_base):
        velocity = step_base.astype(jnp.float32)
        pulled = stencil_x(solve_x_adjoint(velocity[0] * state, *matrices))
        along_y = central_six(velocity[1] * state, 2)
        along_z = central_six(velocity[2] * state, 3)
        return state + time_step * (pulled + along_y + along_z)

    state_one = tangent(direction, base_flow[0])
    state_two = tangent(state_one, base_flow[1])
    adjoint_two = observe(state_two, plane_x, slot_plane, window_inv)
    adjoint_one = adjoint(adjoint_two, base_flow[1]) + observe(state_one, plane_x, slot_plane, window_inv)
    return adjoint(adjoint_one, base_flow[0]) + direction
```

```python
import functools

import jax
import jax.numpy as jnp
from jax import lax
from jax.experimental import pallas as pl
from jax.experimental.pallas import tpu as pltpu
from jax.sharding import PartitionSpec as P

WIN = 8
time_step = 0.15
NEAR = 7.0 / 9.0
FAR = 1.0 / 36.0
C1 = 45.0 / 60.0
C2 = -9.0 / 60.0
C3 = 1.0 / 60.0
MESH = pl.DeviceIdType.MESH
high = lax.Precision.HIGHEST


def weighted(terms):
    chains = [None, None]
    for n, (coef, block) in enumerate(terms):
        part = coef * block
        chains[n % 2] = part if chains[n % 2] is None else chains[n % 2] + part
    return chains[0] if chains[1] is None else chains[0] + chains[1]


def kernel(
    sizes,
    dir_ref, base_ref, inv_ref,
    local_s, in_s, out_s, schur_s, plane_s, slot_s,
    res_ref,
    state_one, state_two, force, acc, rhs, obs, prod_y, prod_z, hbuf,
    yside, xrecv, ysend, yrecv, zsend, zrecv, edge, winrecv, lanes_inv, blocks,
    xs_sem, xr_sem, ys_sem, yr_sem, zs_sem, zr_sem, es_sem, er_sem, ws_sem, wr_sem,
):
    n_gx, n_gy, n_gz = sizes
    gx, gy, gz = lax.axis_index("gx"), lax.axis_index("gy"), lax.axis_index("gz")
    comps, cx, cy, cz = dir_ref.shape
    half = ysend.shape[4]
    owned = inv_ref.shape[0]
    y_next, y_prev = lax.rem(gy + 1, n_gy), lax.rem(gy + n_gy - 1, n_gy)
    z_next, z_prev = lax.rem(gz + 1, n_gz), lax.rem(gz + n_gz - 1, n_gz)

    @pl.when(gx == 0)
    def _():
        xrecv[:, 0] = jnp.zeros(xrecv.shape[:1] + xrecv.shape[2:], jnp.float32)

    @pl.when(gx == n_gx - 1)
    def _():
        xrecv[:, 1] = jnp.zeros(xrecv.shape[:1] + xrecv.shape[2:], jnp.float32)

    barrier = pltpu.get_barrier_semaphore()
    for d in range(1, n_gx):
        pl.semaphore_signal(barrier, device_id={"gx": lax.rem(gx + d, n_gx)}, device_id_type=MESH)
    for q in (y_prev, y_next):
        pl.semaphore_signal(barrier, device_id={"gy": q}, device_id_type=MESH)
    for q in (z_prev, z_next):
        pl.semaphore_signal(barrier, device_id={"gz": q}, device_id_type=MESH)

    def remote(src, dst, send, recv, where):
        return pltpu.make_async_remote_copy(
            src_ref=src, dst_ref=dst, send_sem=send, recv_sem=recv,
            device_id=where, device_id_type=MESH,
        )

    lane = lax.broadcasted_iota(jnp.int32, (comps, cy, cz), 2)
    sub = lax.broadcasted_iota(jnp.int32, (comps, cy, cz), 1)
    in_group = lane % WIN

    def x_copies(r, src):
        right = remote(src.at[:, cx - 2 : cx], xrecv.at[r, 0], xs_sem.at[r, 0], xr_sem.at[r, 0],
                       {"gx": lax.rem(gx + 1, n_gx)})
        left = remote(src.at[:, 0:2], xrecv.at[r, 1], xs_sem.at[r, 1], xr_sem.at[r, 1],
                      {"gx": lax.rem(gx + n_gx - 1, n_gx)})
        return right, left

    def x_start(copies):
        right, left = copies

        @pl.when(gx < n_gx - 1)
        def _():
            right.start()

        @pl.when(gx > 0)
        def _():
            left.start()

    def x_arrived(copies):
        right, left = copies

        @pl.when(gx > 0)
        def _():
            right.wait_recv()

        @pl.when(gx < n_gx - 1)
        def _():
            left.wait_recv()

    def x_sent(copies):
        right, left = copies

        @pl.when(gx < n_gx - 1)
        def _():
            right.wait_send()

        @pl.when(gx > 0)
        def _():
            left.wait_send()

    def y_copies(r):
        return (
            remote(ysend.at[r, 0], yrecv.at[r, 0], ys_sem.at[r, 0], yr_sem.at[r, 0], {"gy": y_prev}),
            remote(ysend.at[r, 1], yrecv.at[r, 1], ys_sem.at[r, 1], yr_sem.at[r, 1], {"gy": y_next}),
        )

    def z_copies(r):
        return (
            remote(zsend.at[r], zrecv.at[r, 0], zs_sem.at[r, 0], zr_sem.at[r, 0], {"gz": z_prev}),
            remote(zsend.at[r], zrecv.at[r, 1], zs_sem.at[r, 1], zr_sem.at[r, 1], {"gz": z_next}),
        )

    def edge_copies(r):
        return tuple(
            remote(edge.at[r, 0], edge.at[r, d], es_sem.at[r, d], er_sem.at[r, d],
                   {"gx": lax.rem(gx + d, n_gx)})
            for d in range(1, n_gx)
        )

    win_copies = tuple(
        remote(inv_ref, winrecv.at[d - 1], ws_sem.at[d], wr_sem.at[d], {"gx": lax.rem(gx + d, n_gx)})
        for d in range(1, n_gx)
    )

    def start(copies):
        for copy in copies:
            copy.start()

    def arrived(copies):
        for copy in copies:
            copy.wait_recv()

    def pack_y(r, src):
        ysend[r, 0] = src[:, :, 0:half, :]
        ysend[r, 1] = src[:, :, cy - half : cy, :]

    def pack_z(r, src):
        packed = None
        for i in range(cx):
            block = src[:, i]
            turned = block if i == 0 else pltpu.roll(block, WIN * i, 2)
            if packed is None:
                packed = turned
            else:
                packed = jnp.where((lane >= WIN * i - 4) & (lane < WIN * i + 4), turned, packed)
        zsend[r] = packed

    def circular_z(block):
        def diff(k):
            return pltpu.roll(block, cz - k, 2) - pltpu.roll(block, k, 2)

        return C1 * diff(1) + C2 * diff(2) + C3 * diff(3)

    def z_fix(r):
        true = jnp.where(in_group < 4, zrecv[r, 0], zrecv[r, 1])
        delta = true - zsend[r]
        low = jnp.where(in_group >= WIN - 3, delta, 0.0)
        top = jnp.where(in_group < 3, delta, 0.0)
        low_fix = -(C1 * pltpu.roll(low, 1, 2) + C2 * pltpu.roll(low, 2, 2) + C3 * pltpu.roll(low, 3, 2))
        top_fix = (C1 * pltpu.roll(top, cz - 1, 2) + C2 * pltpu.roll(top, cz - 2, 2)
                   + C3 * pltpu.roll(top, cz - 3, 2))
        return jnp.where(in_group < 3, low_fix, 0.0) + jnp.where(in_group >= WIN - 3, top_fix, 0.0)

    def z_fix_of(fix, i):
        turned = fix if i == 0 else pltpu.roll(fix, (cz - WIN * i) % cz, 2)
        return jnp.where((lane < 3) | (lane >= cz - 3), turned, 0.0)

    def fill_sides(r):
        yside[:, :, 0:half, :] = yrecv[r, 0]
        yside[:, :, cy - half : cy, :] = yrecv[r, 1]

    def along_y(block, side):
        def diff(k):
            ahead = pltpu.roll(jnp.where(sub < k, side, block), cy - k, 1)
            behind = pltpu.roll(jnp.where(sub >= cy - k, side, block), k, 1)
            return ahead - behind

        return C1 * diff(1) + C2 * diff(2) + C3 * diff(3)

    def stencil_x(src, r, i):
        def row(n):
            if n < 0:
                return xrecv[r, 0, :, n + 2]
            if n >= cx:
                return xrecv[r, 1, :, n - cx]
            return src[:, n]

        return NEAR * (row(i + 1) - row(i - 1)) + FAR * (row(i + 2) - row(i - 2))

    def velocity(n, c, i):
        return base_ref[n, c, i].astype(jnp.float32)[None]

    def fold(blocks8):
        level, m = list(blocks8), 1
        while len(level) > 1:
            keep = (lane & m) == 0
            level = [
                jnp.where(keep, a + pltpu.roll(a, cz - m, 2), b + pltpu.roll(b, m, 2))
                for a, b in zip(level[0::2], level[1::2])
            ]
            m *= 2
        return level[0]

    def unfold(block):
        level, m = [block], WIN // 2
        while m >= 1:
            keep = (lane & m) == 0
            wider = []
            for t in level:
                wider.append(jnp.where(keep, t, pltpu.roll(t, m, 2)))
                wider.append(jnp.where(keep, pltpu.roll(t, cz - m, 2), t))
            level = wider
            m //= 2
        return level

    def observe(src, dst):
        for g in range(cx // WIN):
            sums = fold([src[:, g * WIN + k] for k in range(WIN)])
            mixed = lax.dot_general(
                sums.reshape(comps * cy, cz), blocks[g], (((1,), (1,)), ((), ())),
                precision=high, preferred_element_type=jnp.float32,
            ).reshape(comps, cy, cz)
            for k, t in enumerate(unfold(mixed)):
                dst[:, g * WIN + k] = t

    def build_blocks():
        count = inv_ref.shape[2]
        spread = (
            lax.broadcasted_iota(jnp.int32, (count, cz), 1) // WIN
            == lax.broadcasted_iota(jnp.int32, (count, cz), 0)
        ).astype(jnp.float32)
        for d in range(n_gx):
            source = inv_ref[...] if d == 0 else winrecv[d - 1]
            lanes_inv[d * owned : (d + 1) * owned] = jnp.dot(
                source.reshape(owned * count, count), spread,
                precision=high, preferred_element_type=jnp.float32,
            ).reshape(owned, count, cz) * (1.0 / (WIN * WIN))
        blocks[...] = jnp.zeros(blocks.shape, jnp.float32)
        row = lax.broadcasted_iota(jnp.int32, (WIN, cz), 0)
        col = lax.broadcasted_iota(jnp.int32, (WIN, cz), 1) % WIN

        def add_slot(j, carry):
            owner = lax.rem(gx + n_gx - j // owned, n_gx)
            cell = plane_s[slot_s[owner * owned + j % owned]] - gx * cx
            for g in range(cx // WIN):
                here = (row == cell - g * WIN) & (col == cell - g * WIN)
                for s in range(count):
                    line = jnp.broadcast_to(lanes_inv[j, s : s + 1, :], (WIN, cz))
                    blocks[g, s * WIN : (s + 1) * WIN, :] += jnp.where(here, line, 0.0)
            return carry

        lax.fori_loop(0, n_gx * owned, add_slot, 0)

    def interface(r, m, transposed):
        terms = []
        for d in range(n_gx):
            owner = lax.rem(gx + n_gx - d, n_gx)
            for k in range(2):
                n, own = 2 * owner + k, 2 * gx + m
                coef = schur_s[n, own] if transposed else schur_s[own, n]
                terms.append((coef, edge[r, d, k]))
        return weighted(terms)

    sent = []

    def tangent(r, n, src, dst, first, shadow):
        xc, yc, zc, ec = x_copies(r, src), y_copies(r), z_copies(r), edge_copies(r)
        if not first:
            x_start(xc)
        pack_z(r, src)
        if not first:
            start(zc)
        pack_y(r, src)
        if first:
            pl.semaphore_wait(barrier, n_gx - 1 + 4)
            x_start(xc)
            start(zc)
        start(yc)
        sent.append((xc, yc + zc + ec))
        for i in range(cx):
            block = src[:, i]
            acc[:, i] = block - time_step * (velocity(n, 2, i) * circular_z(block))
        x_arrived(xc)
        for i in range(cx):
            rhs[:, i] = stencil_x(src, r, i)
        for k in range(2):
            edge[r, 0, k] = weighted([(in_s[k, j], rhs[:, j]) for j in range(cx)])
        start(ec)
        if first:
            start(win_copies)
        for i in range(cx):
            solved = weighted([(local_s[i, j], rhs[:, j]) for j in range(cx)])
            acc[:, i] -= time_step * (velocity(n, 0, i) * solved)
        shadow()
        arrived(yc)
        fill_sides(r)
        for i in range(cx):
            acc[:, i] -= time_step * (velocity(n, 1, i) * along_y(src[:, i], yside[:, i]))
        arrived(zc)
        fix = z_fix(r)
        arrived(ec)
        values = [interface(r, m, False) for m in range(2)]
        for i in range(cx):
            pulled = out_s[i, 0] * values[0] + out_s[i, 1] * values[1]
            dst[:, i] = acc[:, i] - time_step * (
                velocity(n, 0, i) * pulled + velocity(n, 2, i) * z_fix_of(fix, i)
            )

    def adjoint(r, n, src, dst, extra):
        xc, yc, zc, ec = x_copies(r, hbuf.at[r - 2]), y_copies(r), z_copies(r), edge_copies(r)
        sent.append((xc, yc + zc + ec))
        held = hbuf.at[r - 2]
        for i in range(cx):
            block = src[:, i]
            rhs[:, i] = velocity(n, 0, i) * block
            prod_y[:, i] = velocity(n, 1, i) * block
            prod_z[:, i] = velocity(n, 2, i) * block
        for k in range(2):
            edge[r, 0, k] = weighted([(out_s[i, k], rhs[:, i]) for i in range(cx)])
        start(ec)
        pack_z(r, prod_z)
        start(zc)
        pack_y(r, prod_y)
        start(yc)
        order = (0, 1, cx - 2, cx - 1) + tuple(range(2, cx - 2))
        for i in order:
            acc[:, i] = weighted([(local_s[j, i], rhs[:, j]) for j in range(cx)])
        arrived(ec)
        values = [interface(r, m, True) for m in range(2)]
        for place, i in enumerate(order):
            held[:, i] = acc[:, i] + (in_s[0, i] * values[0] + in_s[1, i] * values[1])
            if place == 3:
                x_start(xc)
        for i in range(cx):
            total = src[:, i] + time_step * circular_z(prod_z[:, i])
            acc[:, i] = total if extra is None else total + extra[:, i]
        for i in range(2, cx - 2):
            acc[:, i] += time_step * stencil_x(held, r, i)
        arrived(yc)
        fill_sides(r)
        for i in range(cx):
            acc[:, i] += time_step * along_y(prod_y[:, i], yside[:, i])
        arrived(zc)
        fix = z_fix(r)
        x_arrived(xc)
        for i in range(cx):
            total = acc[:, i] + time_step * z_fix_of(fix, i)
            if i < 2 or i >= cx - 2:
                total = total + time_step * stencil_x(held, r, i)
            dst[:, i] = total

    def nothing():
        pass

    def observe_one():
        arrived(win_copies)
        build_blocks()
        observe(state_one, obs)

    tangent(0, 0, dir_ref, state_one, True, nothing)
    tangent(1, 1, state_one, state_two, False, observe_one)
    observe(state_two, force)
    adjoint(2, 1, force, state_two, obs)
    adjoint(3, 0, state_two, res_ref, None)
    for xc, rest in sent:
        x_sent(xc)
        for copy in rest:
            copy.wait_send()
    for copy in win_copies:
        copy.wait_send()


def solution(mesh):
    sizes = tuple(mesh.shape[name] for name in ("gx", "gy", "gz"))

    def local(direction, base_flow, local_inv, couple_in, couple_out, schur_inv,
              plane_x, slot_plane, window_inv):
        n_gx = sizes[0]
        comps, cx, cy, cz = direction.shape
        owned, count = window_inv.shape[0], window_inv.shape[3]
        half = max(3, cy // 2)
        field = pltpu.VMEM(direction.shape, jnp.float32)

        def held(*shape):
            return pltpu.VMEM(shape, jnp.float32)

        sems = pltpu.SemaphoreType.DMA
        vmem = pl.BlockSpec(memory_space=pltpu.VMEM)
        smem = pl.BlockSpec(memory_space=pltpu.SMEM)
        pulled = pl.pallas_call(
            functools.partial(kernel, sizes),
            out_shape=jax.ShapeDtypeStruct(direction.shape, jnp.float32),
            in_specs=[vmem] * 3 + [smem] * 6,
            out_specs=vmem,
            scratch_shapes=[field] * 8 + [
                held(2, comps, cx, cy, cz),
                field,
                held(4, 2, comps, 2, cy, cz),
                held(4, 2, comps, cx, half, cz),
                held(4, 2, comps, cx, half, cz),
                held(4, comps, cy, cz),
                held(4, 2, comps, cy, cz),
                held(4, n_gx, 2, comps, cy, cz),
                held(n_gx - 1, owned, count, count),
                held(n_gx * owned, count, cz),
                held(cx // WIN, count * WIN, cz),
                sems((4, 2)), sems((4, 2)), sems((4, 2)), sems((4, 2)), sems((4, 2)), sems((4, 2)),
                sems((4, n_gx)), sems((4, n_gx)), sems((n_gx,)), sems((n_gx,)),
            ],
            compiler_params=pltpu.CompilerParams(collective_id=0, has_side_effects=True),
        )(
            direction, base_flow, window_inv.reshape(owned, count, count),
            local_inv, couple_in, couple_out, schur_inv, plane_x, slot_plane,
        )
        return pulled + direction

    return jax.shard_map(
        local,
        mesh=mesh,
        in_specs=(
            P(None, "gx", "gy", "gz"),
            P(None, None, "gx", "gy", "gz"),
            P("gx", None),
            P("gx", None),
            P("gx", None),
            P(),
            P(),
            P(),
            P("gx", "gy", "gz", None, None),
        ),
        out_specs=P(None, "gx", "gy", "gz"),
        check_vma=False,
    )
```

```python
import functools

import jax
import jax.numpy as jnp
from jax import lax
from jax.experimental import pallas as pl
from jax.experimental.pallas import tpu as pltpu
from jax.sharding import PartitionSpec as P

WIN = 8
time_step = 0.15
NEAR = 7.0 / 9.0
FAR = 1.0 / 36.0
C1 = 45.0 / 60.0
C2 = -9.0 / 60.0
C3 = 1.0 / 60.0
MESH = pl.DeviceIdType.MESH
high = lax.Precision.HIGHEST


def weighted(terms):
    chains = [None, None]
    for n, (coef, block) in enumerate(terms):
        part = coef * block
        chains[n % 2] = part if chains[n % 2] is None else chains[n % 2] + part
    return chains[0] if chains[1] is None else chains[0] + chains[1]


def kernel(
    sizes,
    dir_hbm, base_hbm, inv_hbm,
    local_h, in_h, out_h, schur_h, plane_h, slot_h,
    res_ref,
    dir_ref, base_ref, inv_ref, local_s, in_s, out_s, schur_s, plane_s, slot_s, load_sem,
    state_one, state_two, force, acc, rhs, obs, prod_y, prod_z, hbuf,
    yside, xrecv, ysend, yrecv, zsend, zrecv, edge, winrecv, lanes_inv, blocks,
    xs_sem, xr_sem, ys_sem, yr_sem, zs_sem, zr_sem, es_sem, er_sem, ws_sem, wr_sem,
):
    n_gx, n_gy, n_gz = sizes
    gx, gy, gz = lax.axis_index("gx"), lax.axis_index("gy"), lax.axis_index("gz")
    comps, cx, cy, cz = dir_ref.shape
    wide = ysend.shape[2]
    loads = [
        pltpu.make_async_copy(src, dst, load_sem.at[n])
        for n, (src, dst) in enumerate((
            (dir_hbm, dir_ref), (in_h, in_s), (schur_h, schur_s), (local_h, local_s),
            (out_h, out_s), (plane_h, plane_s), (slot_h, slot_s),
            (base_hbm, base_ref), (inv_hbm, inv_ref),
        ))
    ]
    owned = inv_ref.shape[0]
    y_next, y_prev = lax.rem(gy + 1, n_gy), lax.rem(gy + n_gy - 1, n_gy)
    z_next, z_prev = lax.rem(gz + 1, n_gz), lax.rem(gz + n_gz - 1, n_gz)

    @pl.when(gx == 0)
    def _():
        xrecv[:, 0] = jnp.zeros(xrecv.shape[:1] + xrecv.shape[2:], jnp.float32)

    @pl.when(gx == n_gx - 1)
    def _():
        xrecv[:, 1] = jnp.zeros(xrecv.shape[:1] + xrecv.shape[2:], jnp.float32)

    barrier = pltpu.get_barrier_semaphore()
    for d in range(1, n_gx):
        pl.semaphore_signal(barrier, device_id={"gx": lax.rem(gx + d, n_gx)}, device_id_type=MESH)
    for q in (y_prev, y_next):
        pl.semaphore_signal(barrier, device_id={"gy": q}, device_id_type=MESH)
    for q in (z_prev, z_next):
        pl.semaphore_signal(barrier, device_id={"gz": q}, device_id_type=MESH)

    for copy in loads:
        copy.start()

    def remote(src, dst, send, recv, where):
        return pltpu.make_async_remote_copy(
            src_ref=src, dst_ref=dst, send_sem=send, recv_sem=recv,
            device_id=where, device_id_type=MESH,
        )

    lane = lax.broadcasted_iota(jnp.int32, (comps, cy, cz), 2)
    sub = lax.broadcasted_iota(jnp.int32, (comps, cy, cz), 1)
    in_group = lane % WIN

    def x_copies(r, src):
        right = remote(src.at[:, cx - 2 : cx], xrecv.at[r, 0], xs_sem.at[r, 0], xr_sem.at[r, 0],
                       {"gx": lax.rem(gx + 1, n_gx)})
        left = remote(src.at[:, 0:2], xrecv.at[r, 1], xs_sem.at[r, 1], xr_sem.at[r, 1],
                      {"gx": lax.rem(gx + n_gx - 1, n_gx)})
        return right, left

    def x_start(copies):
        right, left = copies

        @pl.when(gx < n_gx - 1)
        def _():
            right.start()

        @pl.when(gx > 0)
        def _():
            left.start()

    def x_arrived(copies):
        right, left = copies

        @pl.when(gx > 0)
        def _():
            right.wait_recv()

        @pl.when(gx < n_gx - 1)
        def _():
            left.wait_recv()

    def x_sent(copies):
        right, left = copies

        @pl.when(gx < n_gx - 1)
        def _():
            right.wait_send()

        @pl.when(gx > 0)
        def _():
            left.wait_send()

    def y_copies(r):
        return (
            remote(ysend.at[r, 0], yrecv.at[r, 0], ys_sem.at[r, 0], yr_sem.at[r, 0], {"gy": y_prev}),
            remote(ysend.at[r, 1], yrecv.at[r, 1], ys_sem.at[r, 1], yr_sem.at[r, 1], {"gy": y_next}),
        )

    def z_copies(r):
        return (
            remote(zsend.at[r], zrecv.at[r, 0], zs_sem.at[r, 0], zr_sem.at[r, 0], {"gz": z_prev}),
            remote(zsend.at[r], zrecv.at[r, 1], zs_sem.at[r, 1], zr_sem.at[r, 1], {"gz": z_next}),
        )

    def edge_copies(r):
        return tuple(
            remote(edge.at[r, 0], edge.at[r, d], es_sem.at[r, d], er_sem.at[r, d],
                   {"gx": lax.rem(gx + d, n_gx)})
            for d in range(1, n_gx)
        )

    win_copies = tuple(
        remote(inv_ref, winrecv.at[d - 1], ws_sem.at[d], wr_sem.at[d], {"gx": lax.rem(gx + d, n_gx)})
        for d in range(1, n_gx)
    )

    def start(copies):
        for copy in copies:
            copy.start()

    def arrived(copies):
        for copy in copies:
            copy.wait_recv()

    def pack_y(r, src):
        lines = src.reshape(comps * cx * cy, cz)
        for c in range(comps):
            for m in range(wide):
                for side, row in ((0, m), (1, cy - wide + m)):
                    ysend[r, side, m, c] = lines[pl.ds(c * cx * cy + row, cx, stride=cy), :]

    def pack_z(r, src):
        packed = None
        for i in range(cx):
            block = src[:, i]
            turned = block if i == 0 else pltpu.roll(block, WIN * i, 2)
            if packed is None:
                packed = turned
            else:
                packed = jnp.where((lane >= WIN * i - 4) & (lane < WIN * i + 4), turned, packed)
        zsend[r] = packed

    def circular_z(block):
        def diff(k):
            return pltpu.roll(block, cz - k, 2) - pltpu.roll(block, k, 2)

        return C1 * diff(1) + C2 * diff(2) + C3 * diff(3)

    def z_fix(r):
        true = jnp.where(in_group < 4, zrecv[r, 0], zrecv[r, 1])
        delta = true - zsend[r]
        low = jnp.where(in_group >= WIN - 3, delta, 0.0)
        top = jnp.where(in_group < 3, delta, 0.0)
        low_fix = -(C1 * pltpu.roll(low, 1, 2) + C2 * pltpu.roll(low, 2, 2) + C3 * pltpu.roll(low, 3, 2))
        top_fix = (C1 * pltpu.roll(top, cz - 1, 2) + C2 * pltpu.roll(top, cz - 2, 2)
                   + C3 * pltpu.roll(top, cz - 3, 2))
        return jnp.where(in_group < 3, low_fix, 0.0) + jnp.where(in_group >= WIN - 3, top_fix, 0.0)

    def z_fix_of(fix, i):
        turned = fix if i == 0 else pltpu.roll(fix, (cz - WIN * i) % cz, 2)
        return jnp.where((lane < 3) | (lane >= cz - 3), turned, 0.0)

    def fill_sides(r):
        lines = yside.reshape(comps * cx * cy, cz)
        for c in range(comps):
            for m in range(wide):
                for side, row in ((0, m), (1, cy - wide + m)):
                    lines[pl.ds(c * cx * cy + row, cx, stride=cy), :] = yrecv[r, side, m, c]

    def along_y(block, side):
        def diff(k):
            ahead = pltpu.roll(jnp.where(sub < k, side, block), cy - k, 1)
            behind = pltpu.roll(jnp.where(sub >= cy - k, side, block), k, 1)
            return ahead - behind

        return C1 * diff(1) + C2 * diff(2) + C3 * diff(3)

    def stencil_x(src, r, i):
        def row(n):
            if n < 0:
                return xrecv[r, 0, :, n + 2]
            if n >= cx:
                return xrecv[r, 1, :, n - cx]
            return src[:, n]

        return NEAR * (row(i + 1) - row(i - 1)) + FAR * (row(i + 2) - row(i - 2))

    def velocity(n, c, i):
        return base_ref[n, c, i].astype(jnp.float32)[None]

    def fold(blocks8):
        level, m = list(blocks8), 1
        while len(level) > 1:
            keep = (lane & m) == 0
            level = [
                jnp.where(keep, a + pltpu.roll(a, cz - m, 2), b + pltpu.roll(b, m, 2))
                for a, b in zip(level[0::2], level[1::2])
            ]
            m *= 2
        return level[0]

    def unfold(block):
        level, m = [block], WIN // 2
        while m >= 1:
            keep = (lane & m) == 0
            wider = []
            for t in level:
                wider.append(jnp.where(keep, t, pltpu.roll(t, m, 2)))
                wider.append(jnp.where(keep, pltpu.roll(t, cz - m, 2), t))
            level = wider
            m //= 2
        return level

    def observe(src, dst):
        for g in range(cx // WIN):
            sums = fold([src[:, g * WIN + k] for k in range(WIN)])
            mixed = lax.dot_general(
                sums.reshape(comps * cy, cz), blocks[g], (((1,), (1,)), ((), ())),
                precision=high, preferred_element_type=jnp.float32,
            ).reshape(comps, cy, cz)
            for k, t in enumerate(unfold(mixed)):
                dst[:, g * WIN + k] = t

    def build_blocks():
        count = inv_ref.shape[2]
        spread = (
            lax.broadcasted_iota(jnp.int32, (count, cz), 1) // WIN
            == lax.broadcasted_iota(jnp.int32, (count, cz), 0)
        ).astype(jnp.float32)
        for d in range(n_gx):
            source = inv_ref[...] if d == 0 else winrecv[d - 1]
            lanes_inv[d * owned : (d + 1) * owned] = jnp.dot(
                source.reshape(owned * count, count), spread,
                precision=high, preferred_element_type=jnp.float32,
            ).reshape(owned, count, cz) * (1.0 / (WIN * WIN))
        blocks[...] = jnp.zeros(blocks.shape, jnp.float32)
        row = lax.broadcasted_iota(jnp.int32, (WIN, cz), 0)
        col = lax.broadcasted_iota(jnp.int32, (WIN, cz), 1) % WIN

        def add_slot(j, carry):
            owner = lax.rem(gx + n_gx - j // owned, n_gx)
            cell = plane_s[slot_s[owner * owned + j % owned]] - gx * cx
            for g in range(cx // WIN):
                here = (row == cell - g * WIN) & (col == cell - g * WIN)
                for s in range(count):
                    line = jnp.broadcast_to(lanes_inv[j, s : s + 1, :], (WIN, cz))
                    blocks[g, s * WIN : (s + 1) * WIN, :] += jnp.where(here, line, 0.0)
            return carry

        lax.fori_loop(0, n_gx * owned, add_slot, 0)

    def interface(r, m, transposed):
        terms = []
        for d in range(n_gx):
            owner = lax.rem(gx + n_gx - d, n_gx)
            for k in range(2):
                n, own = 2 * owner + k, 2 * gx + m
                coef = schur_s[n, own] if transposed else schur_s[own, n]
                terms.append((coef, edge[r, d, k]))
        return weighted(terms)

    sent = []

    def tangent(r, n, src, dst, first, shadow):
        xc, yc, zc, ec = x_copies(r, src), y_copies(r), z_copies(r), edge_copies(r)
        if first:
            loads[0].wait()
        else:
            x_start(xc)
        pack_z(r, src)
        if not first:
            start(zc)
        pack_y(r, src)
        if first:
            pl.semaphore_wait(barrier, n_gx - 1 + 4)
            x_start(xc)
            start(zc)
        start(yc)
        sent.append((xc, yc + zc + ec))
        if first:
            for copy in loads[1:]:
                copy.wait()
        for i in range(cx):
            block = src[:, i]
            acc[:, i] = block - time_step * (velocity(n, 2, i) * circular_z(block))
        x_arrived(xc)
        for i in range(cx):
            rhs[:, i] = stencil_x(src, r, i)
        for k in range(2):
            edge[r, 0, k] = weighted([(in_s[k, j], rhs[:, j]) for j in range(cx)])
        start(ec)
        if first:
            start(win_copies)
        for i in range(cx):
            solved = weighted([(local_s[i, j], rhs[:, j]) for j in range(cx)])
            acc[:, i] -= time_step * (velocity(n, 0, i) * solved)
        shadow()
        arrived(yc)
        fill_sides(r)
        for i in range(cx):
            acc[:, i] -= time_step * (velocity(n, 1, i) * along_y(src[:, i], yside[:, i]))
        arrived(zc)
        fix = z_fix(r)
        arrived(ec)
        values = [interface(r, m, False) for m in range(2)]
        for i in range(cx):
            pulled = out_s[0, i] * values[0] + out_s[1, i] * values[1]
            dst[:, i] = acc[:, i] - time_step * (
                velocity(n, 0, i) * pulled + velocity(n, 2, i) * z_fix_of(fix, i)
            )

    def adjoint(r, n, src, dst, extra):
        xc, yc, zc, ec = x_copies(r, hbuf.at[r - 2]), y_copies(r), z_copies(r), edge_copies(r)
        sent.append((xc, yc + zc + ec))
        held = hbuf.at[r - 2]
        for i in range(cx):
            block = src[:, i]
            rhs[:, i] = velocity(n, 0, i) * block
            prod_y[:, i] = velocity(n, 1, i) * block
            prod_z[:, i] = velocity(n, 2, i) * block
        for k in range(2):
            edge[r, 0, k] = weighted([(out_s[k, i], rhs[:, i]) for i in range(cx)])
        start(ec)
        pack_z(r, prod_z)
        start(zc)
        pack_y(r, prod_y)
        start(yc)
        order = (0, 1, cx - 2, cx - 1) + tuple(range(2, cx - 2))
        for i in order:
            acc[:, i] = weighted([(local_s[j, i], rhs[:, j]) for j in range(cx)])
        arrived(ec)
        values = [interface(r, m, True) for m in range(2)]
        for place, i in enumerate(order):
            held[:, i] = acc[:, i] + (in_s[0, i] * values[0] + in_s[1, i] * values[1])
            if place == 3:
                x_start(xc)
        for i in range(cx):
            total = src[:, i] + time_step * circular_z(prod_z[:, i])
            acc[:, i] = total if extra is None else total + extra[:, i]
        for i in range(2, cx - 2):
            acc[:, i] += time_step * stencil_x(held, r, i)
        arrived(yc)
        fill_sides(r)
        for i in range(cx):
            acc[:, i] += time_step * along_y(prod_y[:, i], yside[:, i])
        arrived(zc)
        fix = z_fix(r)
        x_arrived(xc)
        for i in range(cx):
            total = acc[:, i] + time_step * z_fix_of(fix, i)
            if i < 2 or i >= cx - 2:
                total = total + time_step * stencil_x(held, r, i)
            dst[:, i] = total

    def nothing():
        pass

    def observe_one():
        arrived(win_copies)
        build_blocks()
        observe(state_one, obs)

    tangent(0, 0, dir_ref, state_one, True, nothing)
    tangent(1, 1, state_one, state_two, False, observe_one)
    observe(state_two, force)
    adjoint(2, 1, force, state_two, obs)
    adjoint(3, 0, state_two, res_ref, None)
    for xc, rest in sent:
        x_sent(xc)
        for copy in rest:
            copy.wait_send()
    for copy in win_copies:
        copy.wait_send()


def solution(mesh):
    sizes = tuple(mesh.shape[name] for name in ("gx", "gy", "gz"))

    def local(direction, base_flow, local_inv, couple_in, couple_out, schur_inv,
              plane_x, slot_plane, window_inv):
        n_gx = sizes[0]
        comps, cx, cy, cz = direction.shape
        owned, count = window_inv.shape[0], window_inv.shape[3]
        wide = 3
        field = pltpu.VMEM(direction.shape, jnp.float32)

        def held(*shape):
            return pltpu.VMEM(shape, jnp.float32)

        sems = pltpu.SemaphoreType.DMA
        vmem = pl.BlockSpec(memory_space=pltpu.VMEM)
        hbm = pl.BlockSpec(memory_space=pltpu.HBM)
        tables = (local_inv, couple_in, couple_out.T, schur_inv, plane_x, slot_plane)
        pulled = pl.pallas_call(
            functools.partial(kernel, sizes),
            out_shape=jax.ShapeDtypeStruct(direction.shape, jnp.float32),
            in_specs=[hbm] * 9,
            out_specs=vmem,
            scratch_shapes=[
                field, pltpu.VMEM(base_flow.shape, base_flow.dtype), held(owned, count, count),
            ] + [pltpu.SMEM(t.shape, t.dtype) for t in tables] + [sems((9,))] + [field] * 8 + [
                held(2, comps, cx, cy, cz),
                field,
                held(4, 2, comps, 2, cy, cz),
                held(4, 2, wide, comps, cx, cz),
                held(4, 2, wide, comps, cx, cz),
                held(4, comps, cy, cz),
                held(4, 2, comps, cy, cz),
                held(4, n_gx, 2, comps, cy, cz),
                held(n_gx - 1, owned, count, count),
                held(n_gx * owned, count, cz),
                held(cx // WIN, count * WIN, cz),
                sems((4, 2)), sems((4, 2)), sems((4, 2)), sems((4, 2)), sems((4, 2)), sems((4, 2)),
                sems((4, n_gx)), sems((4, n_gx)), sems((n_gx,)), sems((n_gx,)),
            ],
            compiler_params=pltpu.CompilerParams(collective_id=0, has_side_effects=True),
        )(
            direction, base_flow, window_inv.reshape(owned, count, count),
            *tables,
        )
        return pulled + direction

    return jax.shard_map(
        local,
        mesh=mesh,
        in_specs=(
            P(None, "gx", "gy", "gz"),
            P(None, None, "gx", "gy", "gz"),
            P("gx", None),
            P("gx", None),
            P("gx", None),
            P(),
            P(),
            P(),
            P("gx", "gy", "gz", None, None),
        ),
        out_specs=P(None, "gx", "gy", "gz"),
        check_vma=False,
    )
```

```python
import functools

import jax
import jax.numpy as jnp
from jax import lax
from jax.experimental import pallas as pl
from jax.experimental.pallas import tpu as pltpu
from jax.sharding import PartitionSpec as P

WIN = 8
time_step = 0.15
NEAR = 7.0 / 9.0
FAR = 1.0 / 36.0
C1 = 45.0 / 60.0
C2 = -9.0 / 60.0
C3 = 1.0 / 60.0
MESH = pl.DeviceIdType.MESH
high = lax.Precision.HIGHEST


def weighted(terms):
    chains = [None, None]
    for n, (coef, block) in enumerate(terms):
        part = coef * block
        chains[n % 2] = part if chains[n % 2] is None else chains[n % 2] + part
    return chains[0] if chains[1] is None else chains[0] + chains[1]


def kernel(
    sizes,
    dir_hbm, base_hbm, inv_hbm,
    local_h, in_h, out_h, schur_h, plane_h, slot_h,
    res_ref,
    dir_ref, base_ref, inv_ref, local_s, in_s, out_s, schur_s, plane_s, slot_s, in_v, near_v, near_s, esend, halo, load_sem, table_sem, ts_sem, tr_sem,
    state_one, state_two, force, acc, rhs, obs, prod_y, prod_z, hbuf,
    yside, xrecv, ysend, yrecv, zsend, zrecv, edge, winrecv, lanes_inv, blocks,
    xs_sem, xr_sem, ys_sem, yr_sem, zs_sem, zr_sem, es_sem, er_sem, ws_sem, wr_sem,
):
    n_gx, n_gy, n_gz = sizes
    gx, gy, gz = lax.axis_index("gx"), lax.axis_index("gy"), lax.axis_index("gz")
    comps, cx, cy, cz = dir_ref.shape
    wide = ysend.shape[2]
    loads = [
        pltpu.make_async_copy(src, dst, load_sem.at[n])
        for n, (src, dst) in enumerate((
            (dir_hbm, dir_ref), (in_h, in_s), (schur_h, schur_s), (local_h, local_s),
            (out_h, out_s), (plane_h, plane_s), (slot_h, slot_s),
            (base_hbm, base_ref), (inv_hbm, inv_ref), (in_h, in_v),
        ))
    ]
    owned = inv_ref.shape[0]
    y_next, y_prev = lax.rem(gy + 1, n_gy), lax.rem(gy + n_gy - 1, n_gy)
    z_next, z_prev = lax.rem(gz + 1, n_gz), lax.rem(gz + n_gz - 1, n_gz)

    @pl.when(gx == 0)
    def _():
        xrecv[:, 0] = jnp.zeros(xrecv.shape[:1] + xrecv.shape[2:], jnp.float32)

    @pl.when(gx == n_gx - 1)
    def _():
        xrecv[:, 1] = jnp.zeros(xrecv.shape[:1] + xrecv.shape[2:], jnp.float32)

    barrier = pltpu.get_barrier_semaphore()
    for d in range(1, n_gx):
        pl.semaphore_signal(barrier, device_id={"gx": lax.rem(gx + d, n_gx)}, device_id_type=MESH)
    for q in (y_prev, y_next):
        pl.semaphore_signal(barrier, device_id={"gy": q}, device_id_type=MESH)
    for q in (z_prev, z_next):
        pl.semaphore_signal(barrier, device_id={"gz": q}, device_id_type=MESH)

    for copy in loads:
        copy.start()

    def remote(src, dst, send, recv, where):
        return pltpu.make_async_remote_copy(
            src_ref=src, dst_ref=dst, send_sem=send, recv_sem=recv,
            device_id=where, device_id_type=MESH,
        )

    lane = lax.broadcasted_iota(jnp.int32, (comps, cy, cz), 2)
    sub = lax.broadcasted_iota(jnp.int32, (comps, cy, cz), 1)
    in_group = lane % WIN

    def x_copies(r, src):
        right = remote(src.at[:, cx - 2 : cx], xrecv.at[r, 0], xs_sem.at[r, 0], xr_sem.at[r, 0],
                       {"gx": lax.rem(gx + 1, n_gx)})
        left = remote(src.at[:, 0:2], xrecv.at[r, 1], xs_sem.at[r, 1], xr_sem.at[r, 1],
                      {"gx": lax.rem(gx + n_gx - 1, n_gx)})
        return right, left

    def x_start(copies):
        right, left = copies

        @pl.when(gx < n_gx - 1)
        def _():
            right.start()

        @pl.when(gx > 0)
        def _():
            left.start()

    def x_arrived(copies):
        right, left = copies

        @pl.when(gx > 0)
        def _():
            right.wait_recv()

        @pl.when(gx < n_gx - 1)
        def _():
            left.wait_recv()

    def x_sent(copies):
        right, left = copies

        @pl.when(gx < n_gx - 1)
        def _():
            right.wait_send()

        @pl.when(gx > 0)
        def _():
            left.wait_send()

    def y_copies(r):
        return (
            remote(ysend.at[r, 0], yrecv.at[r, 0], ys_sem.at[r, 0], yr_sem.at[r, 0], {"gy": y_prev}),
            remote(ysend.at[r, 1], yrecv.at[r, 1], ys_sem.at[r, 1], yr_sem.at[r, 1], {"gy": y_next}),
        )

    def z_copies(r):
        return (
            remote(zsend.at[r], zrecv.at[r, 0], zs_sem.at[r, 0], zr_sem.at[r, 0], {"gz": z_prev}),
            remote(zsend.at[r], zrecv.at[r, 1], zs_sem.at[r, 1], zr_sem.at[r, 1], {"gz": z_next}),
        )

    def edge_copies(r):
        return tuple(
            remote(edge.at[r, 0], edge.at[r, d], es_sem.at[r, d], er_sem.at[r, d],
                   {"gx": lax.rem(gx + d, n_gx)})
            for d in range(1, n_gx)
        )

    win_copies = tuple(
        remote(inv_ref, winrecv.at[d - 1], ws_sem.at[d], wr_sem.at[d], {"gx": lax.rem(gx + d, n_gx)})
        for d in range(1, n_gx)
    )

    table_copies = (
        remote(in_v, near_v.at[0], ts_sem.at[0], tr_sem.at[0], {"gx": lax.rem(gx + 1, n_gx)}),
        remote(in_v, near_v.at[1], ts_sem.at[1], tr_sem.at[1], {"gx": lax.rem(gx + n_gx - 1, n_gx)}),
    )
    left_one = jnp.where(gx > 0, 1.0, 0.0)
    right_one = jnp.where(gx < n_gx - 1, 1.0, 0.0)
    left_id, right_id = lax.rem(gx + n_gx - 1, n_gx), lax.rem(gx + 1, n_gx)

    def start(copies):
        for copy in copies:
            copy.start()

    def arrived(copies):
        for copy in copies:
            copy.wait_recv()

    def pack_y(r, src):
        lines = src.reshape(comps * cx * cy, cz)
        for c in range(comps):
            for m in range(wide):
                for side, row in ((0, m), (1, cy - wide + m)):
                    ysend[r, side, m, c] = lines[pl.ds(c * cx * cy + row, cx, stride=cy), :]

    def pack_z(r, src):
        packed = None
        for i in range(cx):
            block = src[:, i]
            turned = block if i == 0 else pltpu.roll(block, WIN * i, 2)
            if packed is None:
                packed = turned
            else:
                packed = jnp.where((lane >= WIN * i - 4) & (lane < WIN * i + 4), turned, packed)
        zsend[r] = packed

    def circular_z(block):
        def diff(k):
            return pltpu.roll(block, cz - k, 2) - pltpu.roll(block, k, 2)

        return C1 * diff(1) + C2 * diff(2) + C3 * diff(3)

    def z_fix(r):
        true = jnp.where(in_group < 4, zrecv[r, 0], zrecv[r, 1])
        delta = true - zsend[r]
        low = jnp.where(in_group >= WIN - 3, delta, 0.0)
        top = jnp.where(in_group < 3, delta, 0.0)
        low_fix = -(C1 * pltpu.roll(low, 1, 2) + C2 * pltpu.roll(low, 2, 2) + C3 * pltpu.roll(low, 3, 2))
        top_fix = (C1 * pltpu.roll(top, cz - 1, 2) + C2 * pltpu.roll(top, cz - 2, 2)
                   + C3 * pltpu.roll(top, cz - 3, 2))
        return jnp.where(in_group < 3, low_fix, 0.0) + jnp.where(in_group >= WIN - 3, top_fix, 0.0)

    def z_fix_of(fix, i):
        turned = fix if i == 0 else pltpu.roll(fix, (cz - WIN * i) % cz, 2)
        return jnp.where((lane < 3) | (lane >= cz - 3), turned, 0.0)

    def fill_sides(r):
        lines = yside.reshape(comps * cx * cy, cz)
        for c in range(comps):
            for m in range(wide):
                for side, row in ((0, m), (1, cy - wide + m)):
                    lines[pl.ds(c * cx * cy + row, cx, stride=cy), :] = yrecv[r, side, m, c]

    def along_y(block, side):
        def diff(k):
            ahead = pltpu.roll(jnp.where(sub < k, side, block), cy - k, 1)
            behind = pltpu.roll(jnp.where(sub >= cy - k, side, block), k, 1)
            return ahead - behind

        return C1 * diff(1) + C2 * diff(2) + C3 * diff(3)

    def stencil_x(src, sides, i):
        def row(n):
            if n < 0:
                return sides[0, :, n + 2]
            if n >= cx:
                return sides[1, :, n - cx]
            return src[:, n]

        return NEAR * (row(i + 1) - row(i - 1)) + FAR * (row(i + 2) - row(i - 2))

    def stencil_inside(src, i):
        total = None
        for offset, coef in ((1, NEAR), (-1, -NEAR), (2, FAR), (-2, -FAR)):
            if 0 <= i + offset < cx:
                part = coef * src[:, i + offset]
                total = part if total is None else total + part
        return total

    def velocity(n, c, i):
        return base_ref[n, c, i].astype(jnp.float32)[None]

    def fold(blocks8):
        level, m = list(blocks8), 1
        while len(level) > 1:
            keep = (lane & m) == 0
            level = [
                jnp.where(keep, a + pltpu.roll(a, cz - m, 2), b + pltpu.roll(b, m, 2))
                for a, b in zip(level[0::2], level[1::2])
            ]
            m *= 2
        return level[0]

    def unfold(block):
        level, m = [block], WIN // 2
        while m >= 1:
            keep = (lane & m) == 0
            wider = []
            for t in level:
                wider.append(jnp.where(keep, t, pltpu.roll(t, m, 2)))
                wider.append(jnp.where(keep, pltpu.roll(t, cz - m, 2), t))
            level = wider
            m //= 2
        return level

    def observe(src, dst):
        for g in range(cx // WIN):
            sums = fold([src[:, g * WIN + k] for k in range(WIN)])
            mixed = lax.dot_general(
                sums.reshape(comps * cy, cz), blocks[g], (((1,), (1,)), ((), ())),
                precision=high, preferred_element_type=jnp.float32,
            ).reshape(comps, cy, cz)
            for k, t in enumerate(unfold(mixed)):
                dst[:, g * WIN + k] = t

    def build_blocks():
        count = inv_ref.shape[2]
        spread = (
            lax.broadcasted_iota(jnp.int32, (count, cz), 1) // WIN
            == lax.broadcasted_iota(jnp.int32, (count, cz), 0)
        ).astype(jnp.float32)
        for d in range(n_gx):
            source = inv_ref[...] if d == 0 else winrecv[d - 1]
            lanes_inv[d * owned : (d + 1) * owned] = jnp.dot(
                source.reshape(owned * count, count), spread,
                precision=high, preferred_element_type=jnp.float32,
            ).reshape(owned, count, cz) * (1.0 / (WIN * WIN))
        blocks[...] = jnp.zeros(blocks.shape, jnp.float32)
        row = lax.broadcasted_iota(jnp.int32, (WIN, cz), 0)
        col = lax.broadcasted_iota(jnp.int32, (WIN, cz), 1) % WIN

        def add_slot(j, carry):
            owner = lax.rem(gx + n_gx - j // owned, n_gx)
            cell = plane_s[slot_s[owner * owned + j % owned]] - gx * cx
            for g in range(cx // WIN):
                here = (row == cell - g * WIN) & (col == cell - g * WIN)
                for s in range(count):
                    line = jnp.broadcast_to(lanes_inv[j, s : s + 1, :], (WIN, cz))
                    blocks[g, s * WIN : (s + 1) * WIN, :] += jnp.where(here, line, 0.0)
            return carry

        lax.fori_loop(0, n_gx * owned, add_slot, 0)

    def interface(r, block, m, transposed):
        terms = []
        for d in range(n_gx):
            owner = lax.rem(gx + n_gx - d, n_gx)
            for k in range(2):
                n, own = 2 * owner + k, 2 * block + m
                coef = schur_s[n, own] if transposed else schur_s[own, n]
                terms.append((coef, edge[r, d, k]))
        return weighted(terms)

    def early_copies(r):
        return tuple(
            remote(esend.at[d], edge.at[r, d], es_sem.at[r, d], er_sem.at[r, d],
                   {"gx": lax.rem(gx + d, n_gx)})
            for d in range(1, n_gx)
        )

    def early_shares(r, src):
        for i in range(cx):
            rhs[:, i] = stencil_inside(src, i)
        below = (NEAR * src[:, 0] + FAR * src[:, 1], FAR * src[:, 0])
        above = (-(NEAR * src[:, cx - 1] + FAR * src[:, cx - 2]), -FAR * src[:, cx - 1])
        parts = []
        for k in range(2):
            parts.append((2 * gx + k, weighted([(in_s[k, j], rhs[:, j]) for j in range(cx)])))
            parts.append((2 * right_id + k, right_one * (
                near_s[1, k, 0] * above[0] + near_s[1, k, 1] * above[1])))
            parts.append((2 * left_id + k, left_one * (
                near_s[0, k, cx - 1] * below[0] + near_s[0, k, cx - 2] * below[1])))
        for d in tuple(range(1, n_gx)) + (0,):
            owner = lax.rem(gx + d, n_gx)
            for m in range(2):
                share = weighted([(schur_s[2 * owner + m, n], part) for n, part in parts])
                if d == 0:
                    edge[r, 0, m] = share
                else:
                    esend[d, m] = share

    sent = []

    def tangent(r, n, src, dst, first, shadow):
        xc, yc, zc = x_copies(r, src), y_copies(r), z_copies(r)
        ec = edge_copies(r) if first else early_copies(r)
        if first:
            loads[0].wait()
        else:
            x_start(xc)
        pack_z(r, src)
        if not first:
            start(zc)
        pack_y(r, src)
        if first:
            pl.semaphore_wait(barrier, n_gx - 1 + 4)
            x_start(xc)
            start(zc)
        start(yc)
        if not first:
            early_shares(r, src)
            start(ec)
        sent.append((xc, yc + zc + ec))
        if first:
            for copy in loads[1:]:
                copy.wait()
            start(table_copies)
        for i in range(cx):
            block = src[:, i]
            acc[:, i] = block - time_step * (velocity(n, 2, i) * circular_z(block))
        x_arrived(xc)
        for i in range(cx) if first else (0, 1, cx - 2, cx - 1):
            rhs[:, i] = stencil_x(src, xrecv.at[r], i)
        if first:
            for k in range(2):
                edge[r, 0, k] = weighted([(in_s[k, j], rhs[:, j]) for j in range(cx)])
            start(ec)
            start(win_copies)
        for i in range(cx):
            solved = weighted([(local_s[i, j], rhs[:, j]) for j in range(cx)])
            acc[:, i] -= time_step * (velocity(n, 0, i) * solved)
        if first:
            arrived(table_copies)
            table = pltpu.make_async_copy(near_v, near_s, table_sem.at[0])
            table.start()
            table.wait()
        shadow()
        arrived(yc)
        fill_sides(r)
        for i in range(cx):
            acc[:, i] -= time_step * (velocity(n, 1, i) * along_y(src[:, i], yside[:, i]))
        arrived(zc)
        fix = z_fix(r)
        arrived(ec)
        if first:
            values = [interface(r, gx, m, False) for m in range(2)]
        else:
            values = [weighted([(1.0, edge[r, d, m]) for d in range(n_gx)]) for m in range(2)]
        for i in range(cx):
            pulled = out_s[0, i] * values[0] + out_s[1, i] * values[1]
            dst[:, i] = acc[:, i] - time_step * (
                velocity(n, 0, i) * pulled + velocity(n, 2, i) * z_fix_of(fix, i)
            )

    def adjoint(r, n, src, dst, extra):
        xc, yc, zc, ec = x_copies(r, hbuf.at[r - 2]), y_copies(r), z_copies(r), edge_copies(r)
        sent.append((xc, yc + zc + ec))
        held = hbuf.at[r - 2]
        for i in range(cx):
            block = src[:, i]
            rhs[:, i] = velocity(n, 0, i) * block
            prod_y[:, i] = velocity(n, 1, i) * block
            prod_z[:, i] = velocity(n, 2, i) * block
        for k in range(2):
            edge[r, 0, k] = weighted([(out_s[k, i], rhs[:, i]) for i in range(cx)])
        start(ec)
        pack_z(r, prod_z)
        start(zc)
        pack_y(r, prod_y)
        start(yc)
        order = (0, 1, cx - 2, cx - 1) + tuple(range(2, cx - 2))
        for place, i in enumerate(order):
            held[:, i] = weighted([(local_s[j, i], rhs[:, j]) for j in range(cx)])
            if place == 3:
                x_start(xc)
        for i in range(cx):
            total = src[:, i] + time_step * circular_z(prod_z[:, i])
            acc[:, i] = total if extra is None else total + extra[:, i]
        arrived(ec)
        values = [interface(r, gx, m, True) for m in range(2)]
        lower = [left_one * interface(r, left_id, m, True) for m in range(2)]
        upper = [right_one * interface(r, right_id, m, True) for m in range(2)]
        for i in range(cx):
            rhs[:, i] = held[:, i] + (in_s[0, i] * values[0] + in_s[1, i] * values[1])
        for i in range(2, cx - 2):
            acc[:, i] += time_step * stencil_x(rhs, halo, i)
        x_arrived(xc)
        for n in range(2):
            halo[0, :, n] = xrecv[r, 0, :, n] + (
                near_s[0, 0, cx - 2 + n] * lower[0] + near_s[0, 1, cx - 2 + n] * lower[1])
            halo[1, :, n] = xrecv[r, 1, :, n] + (
                near_s[1, 0, n] * upper[0] + near_s[1, 1, n] * upper[1])
        for i in (0, 1, cx - 2, cx - 1):
            acc[:, i] += time_step * stencil_x(rhs, halo, i)
        arrived(yc)
        fill_sides(r)
        for i in range(cx):
            acc[:, i] += time_step * along_y(prod_y[:, i], yside[:, i])
        arrived(zc)
        fix = z_fix(r)
        for i in range(cx):
            dst[:, i] = acc[:, i] + time_step * z_fix_of(fix, i)

    def nothing():
        pass

    def observe_one():
        arrived(win_copies)
        build_blocks()
        observe(state_one, obs)

    tangent(0, 0, dir_ref, state_one, True, nothing)
    tangent(1, 1, state_one, state_two, False, observe_one)
    observe(state_two, force)
    adjoint(2, 1, force, state_two, obs)
    adjoint(3, 0, state_two, res_ref, None)
    for xc, rest in sent:
        x_sent(xc)
        for copy in rest:
            copy.wait_send()
    for copy in win_copies + table_copies:
        copy.wait_send()


def solution(mesh):
    sizes = tuple(mesh.shape[name] for name in ("gx", "gy", "gz"))

    def local(direction, base_flow, local_inv, couple_in, couple_out, schur_inv,
              plane_x, slot_plane, window_inv):
        n_gx = sizes[0]
        comps, cx, cy, cz = direction.shape
        owned, count = window_inv.shape[0], window_inv.shape[3]
        wide = 3
        field = pltpu.VMEM(direction.shape, jnp.float32)

        def held(*shape):
            return pltpu.VMEM(shape, jnp.float32)

        sems = pltpu.SemaphoreType.DMA
        vmem = pl.BlockSpec(memory_space=pltpu.VMEM)
        hbm = pl.BlockSpec(memory_space=pltpu.HBM)
        tables = (local_inv, couple_in, couple_out.T, schur_inv, plane_x, slot_plane)
        pulled = pl.pallas_call(
            functools.partial(kernel, sizes),
            out_shape=jax.ShapeDtypeStruct(direction.shape, jnp.float32),
            in_specs=[hbm] * 9,
            out_specs=vmem,
            scratch_shapes=[
                field, pltpu.VMEM(base_flow.shape, base_flow.dtype), held(owned, count, count),
            ] + [pltpu.SMEM(t.shape, t.dtype) for t in tables] + [
                held(2, cx), held(2, 2, cx), pltpu.SMEM((2, 2, cx), jnp.float32),
                held(n_gx, 2, comps, cy, cz), held(2, comps, 2, cy, cz),
                sems((10,)), sems((1,)), sems((2,)), sems((2,)),
            ] + [field] * 8 + [
                held(2, comps, cx, cy, cz),
                field,
                held(4, 2, comps, 2, cy, cz),
                held(4, 2, wide, comps, cx, cz),
                held(4, 2, wide, comps, cx, cz),
                held(4, comps, cy, cz),
                held(4, 2, comps, cy, cz),
                held(4, n_gx, 2, comps, cy, cz),
                held(n_gx - 1, owned, count, count),
                held(n_gx * owned, count, cz),
                held(cx // WIN, count * WIN, cz),
                sems((4, 2)), sems((4, 2)), sems((4, 2)), sems((4, 2)), sems((4, 2)), sems((4, 2)),
                sems((4, n_gx)), sems((4, n_gx)), sems((n_gx,)), sems((n_gx,)),
            ],
            compiler_params=pltpu.CompilerParams(collective_id=0, has_side_effects=True),
        )(
            direction, base_flow, window_inv.reshape(owned, count, count),
            *tables,
        )
        return pulled + direction

    return jax.shard_map(
        local,
        mesh=mesh,
        in_specs=(
            P(None, "gx", "gy", "gz"),
            P(None, None, "gx", "gy", "gz"),
            P("gx", None),
            P("gx", None),
            P("gx", None),
            P(),
            P(),
            P(),
            P("gx", "gy", "gz", None, None),
        ),
        out_specs=P(None, "gx", "gy", "gz"),
        check_vma=False,
    )
```

```python
import functools

import jax
import jax.numpy as jnp
from jax import lax
from jax.experimental import pallas as pl
from jax.experimental.pallas import tpu as pltpu
from jax.sharding import PartitionSpec as P

WIN = 8
time_step = 0.15
NEAR = 7.0 / 9.0
FAR = 1.0 / 36.0
C1 = 45.0 / 60.0
C2 = -9.0 / 60.0
C3 = 1.0 / 60.0
MESH = pl.DeviceIdType.MESH
high = lax.Precision.HIGHEST


def weighted(terms):
    chains = [None, None]
    for n, (coef, block) in enumerate(terms):
        part = coef * block
        chains[n % 2] = part if chains[n % 2] is None else chains[n % 2] + part
    return chains[0] if chains[1] is None else chains[0] + chains[1]


def kernel(
    sizes,
    dir_hbm, base_hbm, inv_hbm,
    local_h, in_h, out_h, schur_h, plane_h, slot_h,
    res_ref,
    dir_ref, base_ref, inv_ref, local_s, in_s, out_s, schur_s, plane_s, slot_s, in_v, near_v, near_s, esend, halo, load_sem, table_sem, ts_sem, tr_sem,
    state_one, state_two, force, acc, rhs, obs, prod_y, prod_z, hbuf,
    yside, xrecv, ysend, yrecv, zsend, zrecv, edge, winrecv, lanes_inv, blocks,
    xs_sem, xr_sem, ys_sem, yr_sem, zs_sem, zr_sem, es_sem, er_sem, ws_sem, wr_sem,
):
    n_gx, n_gy, n_gz = sizes
    gx, gy, gz = lax.axis_index("gx"), lax.axis_index("gy"), lax.axis_index("gz")
    comps, cx, cy, cz = dir_ref.shape
    wide = ysend.shape[2]
    loads = [
        pltpu.make_async_copy(src, dst, load_sem.at[n])
        for n, (src, dst) in enumerate((
            (dir_hbm, dir_ref), (in_h, in_s), (schur_h, schur_s), (local_h, local_s),
            (out_h, out_s), (plane_h, plane_s), (slot_h, slot_s),
            (base_hbm, base_ref), (inv_hbm, inv_ref), (in_h, in_v),
        ))
    ]
    owned = inv_ref.shape[0]
    y_next, y_prev = lax.rem(gy + 1, n_gy), lax.rem(gy + n_gy - 1, n_gy)
    z_next, z_prev = lax.rem(gz + 1, n_gz), lax.rem(gz + n_gz - 1, n_gz)

    @pl.when(gx == 0)
    def _():
        xrecv[:, 0] = jnp.zeros(xrecv.shape[:1] + xrecv.shape[2:], jnp.float32)

    @pl.when(gx == n_gx - 1)
    def _():
        xrecv[:, 1] = jnp.zeros(xrecv.shape[:1] + xrecv.shape[2:], jnp.float32)

    barrier = pltpu.get_barrier_semaphore()
    for d in range(1, n_gx):
        pl.semaphore_signal(barrier, device_id={"gx": lax.rem(gx + d, n_gx)}, device_id_type=MESH)
    for q in (y_prev, y_next):
        pl.semaphore_signal(barrier, device_id={"gy": q}, device_id_type=MESH)
    for q in (z_prev, z_next):
        pl.semaphore_signal(barrier, device_id={"gz": q}, device_id_type=MESH)

    for copy in loads:
        copy.start()

    def remote(src, dst, send, recv, where):
        return pltpu.make_async_remote_copy(
            src_ref=src, dst_ref=dst, send_sem=send, recv_sem=recv,
            device_id=where, device_id_type=MESH,
        )

    lane = lax.broadcasted_iota(jnp.int32, (comps, cy, cz), 2)
    sub = lax.broadcasted_iota(jnp.int32, (comps, cy, cz), 1)
    in_group = lane % WIN

    def x_copies(r, src):
        right = remote(src.at[:, cx - 2 : cx], xrecv.at[r, 0], xs_sem.at[r, 0], xr_sem.at[r, 0],
                       {"gx": lax.rem(gx + 1, n_gx)})
        left = remote(src.at[:, 0:2], xrecv.at[r, 1], xs_sem.at[r, 1], xr_sem.at[r, 1],
                      {"gx": lax.rem(gx + n_gx - 1, n_gx)})
        return right, left

    def x_start(copies):
        right, left = copies

        @pl.when(gx < n_gx - 1)
        def _():
            right.start()

        @pl.when(gx > 0)
        def _():
            left.start()

    def x_arrived(copies):
        right, left = copies

        @pl.when(gx > 0)
        def _():
            right.wait_recv()

        @pl.when(gx < n_gx - 1)
        def _():
            left.wait_recv()

    def x_sent(copies):
        right, left = copies

        @pl.when(gx < n_gx - 1)
        def _():
            right.wait_send()

        @pl.when(gx > 0)
        def _():
            left.wait_send()

    def y_copies(r):
        return (
            remote(ysend.at[r, 0], yrecv.at[r, 0], ys_sem.at[r, 0], yr_sem.at[r, 0], {"gy": y_prev}),
            remote(ysend.at[r, 1], yrecv.at[r, 1], ys_sem.at[r, 1], yr_sem.at[r, 1], {"gy": y_next}),
        )

    def z_copies(r):
        return (
            remote(zsend.at[r], zrecv.at[r, 0], zs_sem.at[r, 0], zr_sem.at[r, 0], {"gz": z_prev}),
            remote(zsend.at[r], zrecv.at[r, 1], zs_sem.at[r, 1], zr_sem.at[r, 1], {"gz": z_next}),
        )

    def edge_copies(r):
        return tuple(
            remote(edge.at[r, 0], edge.at[r, d], es_sem.at[r, d], er_sem.at[r, d],
                   {"gx": lax.rem(gx + d, n_gx)})
            for d in range(1, n_gx)
        )

    win_copies = tuple(
        remote(inv_ref, winrecv.at[d - 1], ws_sem.at[d], wr_sem.at[d], {"gx": lax.rem(gx + d, n_gx)})
        for d in range(1, n_gx)
    )

    table_copies = (
        remote(in_v, near_v.at[0], ts_sem.at[0], tr_sem.at[0], {"gx": lax.rem(gx + 1, n_gx)}),
        remote(in_v, near_v.at[1], ts_sem.at[1], tr_sem.at[1], {"gx": lax.rem(gx + n_gx - 1, n_gx)}),
    )
    left_one = jnp.where(gx > 0, 1.0, 0.0)
    right_one = jnp.where(gx < n_gx - 1, 1.0, 0.0)
    left_id, right_id = lax.rem(gx + n_gx - 1, n_gx), lax.rem(gx + 1, n_gx)

    def start(copies):
        for copy in copies:
            copy.start()

    def arrived(copies):
        for copy in copies:
            copy.wait_recv()

    def pack_y(r, src):
        lines = src.reshape(comps * cx * cy, cz)
        for c in range(comps):
            for m in range(wide):
                for side, row in ((0, m), (1, cy - wide + m)):
                    ysend[r, side, m, c] = lines[pl.ds(c * cx * cy + row, cx, stride=cy), :]

    def pack_z(r, src):
        packed = None
        for i in range(cx):
            block = src[:, i]
            turned = block if i == 0 else pltpu.roll(block, WIN * i, 2)
            if packed is None:
                packed = turned
            else:
                packed = jnp.where((lane >= WIN * i - 4) & (lane < WIN * i + 4), turned, packed)
        zsend[r] = packed

    def circular_z(block):
        def diff(k):
            return pltpu.roll(block, cz - k, 2) - pltpu.roll(block, k, 2)

        return C1 * diff(1) + C2 * diff(2) + C3 * diff(3)

    def z_fix(r):
        true = jnp.where(in_group < 4, zrecv[r, 0], zrecv[r, 1])
        delta = true - zsend[r]
        low = jnp.where(in_group >= WIN - 3, delta, 0.0)
        top = jnp.where(in_group < 3, delta, 0.0)
        low_fix = -(C1 * pltpu.roll(low, 1, 2) + C2 * pltpu.roll(low, 2, 2) + C3 * pltpu.roll(low, 3, 2))
        top_fix = (C1 * pltpu.roll(top, cz - 1, 2) + C2 * pltpu.roll(top, cz - 2, 2)
                   + C3 * pltpu.roll(top, cz - 3, 2))
        return jnp.where(in_group < 3, low_fix, 0.0) + jnp.where(in_group >= WIN - 3, top_fix, 0.0)

    def z_fix_of(fix, i):
        turned = fix if i == 0 else pltpu.roll(fix, (cz - WIN * i) % cz, 2)
        return jnp.where((lane < 3) | (lane >= cz - 3), turned, 0.0)

    def fill_sides(r):
        lines = yside.reshape(comps * cx * cy, cz)
        for c in range(comps):
            for m in range(wide):
                for side, row in ((0, m), (1, cy - wide + m)):
                    lines[pl.ds(c * cx * cy + row, cx, stride=cy), :] = yrecv[r, side, m, c]

    def along_y(block, side):
        def diff(k):
            ahead = pltpu.roll(jnp.where(sub < k, side, block), cy - k, 1)
            behind = pltpu.roll(jnp.where(sub >= cy - k, side, block), k, 1)
            return ahead - behind

        return C1 * diff(1) + C2 * diff(2) + C3 * diff(3)

    def stencil_x(src, sides, i):
        def row(n):
            if n < 0:
                return sides[0, :, n + 2]
            if n >= cx:
                return sides[1, :, n - cx]
            return src[:, n]

        return NEAR * (row(i + 1) - row(i - 1)) + FAR * (row(i + 2) - row(i - 2))

    def stencil_inside(src, i):
        total = None
        for offset, coef in ((1, NEAR), (-1, -NEAR), (2, FAR), (-2, -FAR)):
            if 0 <= i + offset < cx:
                part = coef * src[:, i + offset]
                total = part if total is None else total + part
        return total

    def velocity(n, c, i):
        return base_ref[n, c, i].astype(jnp.float32)[None]

    def fold(blocks8):
        level, m = list(blocks8), 1
        while len(level) > 1:
            keep = (lane & m) == 0
            level = [
                jnp.where(keep, a + pltpu.roll(a, cz - m, 2), b + pltpu.roll(b, m, 2))
                for a, b in zip(level[0::2], level[1::2])
            ]
            m *= 2
        return level[0]

    def unfold(block):
        level, m = [block], WIN // 2
        while m >= 1:
            keep = (lane & m) == 0
            wider = []
            for t in level:
                wider.append(jnp.where(keep, t, pltpu.roll(t, m, 2)))
                wider.append(jnp.where(keep, pltpu.roll(t, cz - m, 2), t))
            level = wider
            m //= 2
        return level

    def observe(src, dst):
        for g in range(cx // WIN):
            sums = fold([src[:, g * WIN + k] for k in range(WIN)])
            mixed = lax.dot_general(
                sums.reshape(comps * cy, cz), blocks[g], (((1,), (1,)), ((), ())),
                precision=high, preferred_element_type=jnp.float32,
            ).reshape(comps, cy, cz)
            for k, t in enumerate(unfold(mixed)):
                dst[:, g * WIN + k] = t

    def build_blocks():
        count = inv_ref.shape[2]
        spread = (
            lax.broadcasted_iota(jnp.int32, (count, cz), 1) // WIN
            == lax.broadcasted_iota(jnp.int32, (count, cz), 0)
        ).astype(jnp.float32)
        for d in range(n_gx):
            source = inv_ref[...] if d == 0 else winrecv[d - 1]
            lanes_inv[d * owned : (d + 1) * owned] = jnp.dot(
                source.reshape(owned * count, count), spread,
                precision=high, preferred_element_type=jnp.float32,
            ).reshape(owned, count, cz) * (1.0 / (WIN * WIN))
        blocks[...] = jnp.zeros(blocks.shape, jnp.float32)
        row = lax.broadcasted_iota(jnp.int32, (WIN, cz), 0)
        col = lax.broadcasted_iota(jnp.int32, (WIN, cz), 1) % WIN

        def add_slot(j, carry):
            owner = lax.rem(gx + n_gx - j // owned, n_gx)
            cell = plane_s[slot_s[owner * owned + j % owned]] - gx * cx
            for g in range(cx // WIN):
                here = (row == cell - g * WIN) & (col == cell - g * WIN)
                for s in range(count):
                    line = jnp.broadcast_to(lanes_inv[j, s : s + 1, :], (WIN, cz))
                    blocks[g, s * WIN : (s + 1) * WIN, :] += jnp.where(here, line, 0.0)
            return carry

        lax.fori_loop(0, n_gx * owned, add_slot, 0)

    def interface(r, block, m, transposed):
        terms = []
        for d in range(n_gx):
            owner = lax.rem(gx + n_gx - d, n_gx)
            for k in range(2):
                n, own = 2 * owner + k, 2 * block + m
                coef = schur_s[n, own] if transposed else schur_s[own, n]
                terms.append((coef, edge[r, d, k]))
        return weighted(terms)

    def early_copies(r):
        return tuple(
            remote(esend.at[d], edge.at[r, d], es_sem.at[r, d], er_sem.at[r, d],
                   {"gx": lax.rem(gx + d, n_gx)})
            for d in range(1, n_gx)
        )

    def early_shares(r, src):
        for i in range(cx):
            rhs[:, i] = stencil_inside(src, i)
        below = (NEAR * src[:, 0] + FAR * src[:, 1], FAR * src[:, 0])
        above = (-(NEAR * src[:, cx - 1] + FAR * src[:, cx - 2]), -FAR * src[:, cx - 1])
        parts = []
        for k in range(2):
            parts.append((2 * gx + k, weighted([(in_s[k, j], rhs[:, j]) for j in range(cx)])))
            parts.append((2 * right_id + k, right_one * (
                near_s[1, k, 0] * above[0] + near_s[1, k, 1] * above[1])))
            parts.append((2 * left_id + k, left_one * (
                near_s[0, k, cx - 1] * below[0] + near_s[0, k, cx - 2] * below[1])))
        for d in tuple(range(1, n_gx)) + (0,):
            owner = lax.rem(gx + d, n_gx)
            for m in range(2):
                share = weighted([(schur_s[2 * owner + m, n], part) for n, part in parts])
                if d == 0:
                    edge[r, 0, m] = share
                else:
                    esend[d, m] = share

    sent = []

    def tangent(r, n, src, dst, first, shadow):
        xc, yc, zc = x_copies(r, src), y_copies(r), z_copies(r)
        ec = edge_copies(r) if first else early_copies(r)
        if first:
            loads[0].wait()
        else:
            x_start(xc)
        pack_z(r, src)
        if not first:
            start(zc)
        pack_y(r, src)
        if first:
            pl.semaphore_wait(barrier, n_gx - 1 + 4)
            x_start(xc)
            start(zc)
        start(yc)
        if not first:
            early_shares(r, src)
            start(ec)
        sent.append((xc, yc + zc + ec))
        if first:
            for copy in loads[1:]:
                copy.wait()
            start(table_copies)
        for i in range(cx):
            block = src[:, i]
            acc[:, i] = block - time_step * (velocity(n, 2, i) * circular_z(block))
        x_arrived(xc)
        for i in range(cx) if first else (0, 1, cx - 2, cx - 1):
            rhs[:, i] = stencil_x(src, xrecv.at[r], i)
        if first:
            for k in range(2):
                edge[r, 0, k] = weighted([(in_s[k, j], rhs[:, j]) for j in range(cx)])
            start(ec)
            start(win_copies)
        for i in range(cx):
            solved = weighted([(local_s[i, j], rhs[:, j]) for j in range(cx)])
            acc[:, i] -= time_step * (velocity(n, 0, i) * solved)
        if first:
            arrived(table_copies)
            table = pltpu.make_async_copy(near_v, near_s, table_sem.at[0])
            table.start()
            table.wait()
        shadow()
        arrived(yc)
        fill_sides(r)
        for i in range(cx):
            acc[:, i] -= time_step * (velocity(n, 1, i) * along_y(src[:, i], yside[:, i]))
        arrived(zc)
        fix = z_fix(r)
        arrived(ec)
        if first:
            values = [interface(r, gx, m, False) for m in range(2)]
        else:
            values = [weighted([(1.0, edge[r, d, m]) for d in range(n_gx)]) for m in range(2)]
        for i in range(cx):
            pulled = out_s[0, i] * values[0] + out_s[1, i] * values[1]
            dst[:, i] = acc[:, i] - time_step * (
                velocity(n, 0, i) * pulled + velocity(n, 2, i) * z_fix_of(fix, i)
            )

    def adjoint(r, n, src, dst, extra):
        xc, yc, zc, ec = x_copies(r, hbuf.at[r - 2]), y_copies(r), z_copies(r), edge_copies(r)
        sent.append((xc, yc + zc + ec))
        held = hbuf.at[r - 2]
        for i in range(cx):
            prod_z[:, i] = velocity(n, 2, i) * src[:, i]
        pack_z(r, prod_z)
        start(zc)
        for i in range(cx):
            prod_y[:, i] = velocity(n, 1, i) * src[:, i]
        pack_y(r, prod_y)
        start(yc)
        for i in range(cx):
            rhs[:, i] = velocity(n, 0, i) * src[:, i]
        for k in range(2):
            edge[r, 0, k] = weighted([(out_s[k, i], rhs[:, i]) for i in range(cx)])
        start(ec)
        order = (0, 1, cx - 2, cx - 1) + tuple(range(2, cx - 2))
        for place, i in enumerate(order):
            held[:, i] = weighted([(local_s[j, i], rhs[:, j]) for j in range(cx)])
            if place == 3:
                x_start(xc)
        for i in range(cx):
            total = src[:, i] + time_step * circular_z(prod_z[:, i])
            acc[:, i] = total if extra is None else total + extra[:, i]
        arrived(ec)
        values = [interface(r, gx, m, True) for m in range(2)]
        lower = [left_one * interface(r, left_id, m, True) for m in range(2)]
        upper = [right_one * interface(r, right_id, m, True) for m in range(2)]
        for i in range(cx):
            rhs[:, i] = held[:, i] + (in_s[0, i] * values[0] + in_s[1, i] * values[1])
        for i in range(2, cx - 2):
            acc[:, i] += time_step * stencil_x(rhs, halo, i)
        x_arrived(xc)
        for n in range(2):
            halo[0, :, n] = xrecv[r, 0, :, n] + (
                near_s[0, 0, cx - 2 + n] * lower[0] + near_s[0, 1, cx - 2 + n] * lower[1])
            halo[1, :, n] = xrecv[r, 1, :, n] + (
                near_s[1, 0, n] * upper[0] + near_s[1, 1, n] * upper[1])
        for i in (0, 1, cx - 2, cx - 1):
            acc[:, i] += time_step * stencil_x(rhs, halo, i)
        arrived(yc)
        fill_sides(r)
        for i in range(cx):
            acc[:, i] += time_step * along_y(prod_y[:, i], yside[:, i])
        arrived(zc)
        fix = z_fix(r)
        for i in range(cx):
            dst[:, i] = acc[:, i] + time_step * z_fix_of(fix, i)

    def nothing():
        pass

    def observe_one():
        arrived(win_copies)
        build_blocks()
        observe(state_one, obs)

    tangent(0, 0, dir_ref, state_one, True, nothing)
    tangent(1, 1, state_one, state_two, False, observe_one)
    observe(state_two, force)
    adjoint(2, 1, force, state_two, obs)
    adjoint(3, 0, state_two, res_ref, None)
    for xc, rest in sent:
        x_sent(xc)
        for copy in rest:
            copy.wait_send()
    for copy in win_copies + table_copies:
        copy.wait_send()


def solution(mesh):
    sizes = tuple(mesh.shape[name] for name in ("gx", "gy", "gz"))

    def local(direction, base_flow, local_inv, couple_in, couple_out, schur_inv,
              plane_x, slot_plane, window_inv):
        n_gx = sizes[0]
        comps, cx, cy, cz = direction.shape
        owned, count = window_inv.shape[0], window_inv.shape[3]
        wide = 3
        field = pltpu.VMEM(direction.shape, jnp.float32)

        def held(*shape):
            return pltpu.VMEM(shape, jnp.float32)

        sems = pltpu.SemaphoreType.DMA
        vmem = pl.BlockSpec(memory_space=pltpu.VMEM)
        kept = functools.partial(pltpu.with_memory_space_constraint, memory_space=pltpu.HBM)
        hbm = pl.BlockSpec(memory_space=pltpu.HBM)
        tables = (local_inv, couple_in, couple_out.T, schur_inv, plane_x, slot_plane)
        pulled = pl.pallas_call(
            functools.partial(kernel, sizes),
            out_shape=jax.ShapeDtypeStruct(direction.shape, jnp.float32),
            in_specs=[hbm] * 9,
            out_specs=vmem,
            scratch_shapes=[
                field, pltpu.VMEM(base_flow.shape, base_flow.dtype), held(owned, count, count),
            ] + [pltpu.SMEM(t.shape, t.dtype) for t in tables] + [
                held(2, cx), held(2, 2, cx), pltpu.SMEM((2, 2, cx), jnp.float32),
                held(n_gx, 2, comps, cy, cz), held(2, comps, 2, cy, cz),
                sems((10,)), sems((1,)), sems((2,)), sems((2,)),
            ] + [field] * 8 + [
                held(2, comps, cx, cy, cz),
                field,
                held(4, 2, comps, 2, cy, cz),
                held(4, 2, wide, comps, cx, cz),
                held(4, 2, wide, comps, cx, cz),
                held(4, comps, cy, cz),
                held(4, 2, comps, cy, cz),
                held(4, n_gx, 2, comps, cy, cz),
                held(n_gx - 1, owned, count, count),
                held(n_gx * owned, count, cz),
                held(cx // WIN, count * WIN, cz),
                sems((4, 2)), sems((4, 2)), sems((4, 2)), sems((4, 2)), sems((4, 2)), sems((4, 2)),
                sems((4, n_gx)), sems((4, n_gx)), sems((n_gx,)), sems((n_gx,)),
            ],
            compiler_params=pltpu.CompilerParams(collective_id=0, has_side_effects=True, vmem_limit_bytes=16 * 2**20),
        )(
            *map(kept, (direction, base_flow, window_inv.reshape(owned, count, count)) + tables),
        )
        return pulled + direction

    return jax.shard_map(
        local,
        mesh=mesh,
        in_specs=(
            P(None, "gx", "gy", "gz"),
            P(None, None, "gx", "gy", "gz"),
            P("gx", None),
            P("gx", None),
            P("gx", None),
            P(),
            P(),
            P(),
            P("gx", "gy", "gz", None, None),
        ),
        out_specs=P(None, "gx", "gy", "gz"),
        check_vma=False,
    )
```
